512 devices in a mesh: lat: 16 (over z_hi, y), lon: 32 (over z_lo, x, core).
Axes of the slice: x: 4, y: 4, z: 16 (z_hi: 4, z_lo: 4; z = z_hi * 4 + z_lo), core: 2. Of those that a mesh axis runs over, the one named last changes fastest.
Arguments:
- height: float32 [3072, 12288], P('lat', 'lon'), may hold values from -6 to 6
- flux_lon: float32 [3072, 12288], P('lat', 'lon'), may hold values from -4 to 4
- flux_lat: float32 [3072, 12288], P('lat', 'lon'), may hold values from -4 to 4
- depth: float32 [3072, 12288], P('lat', 'lon'), may hold values from 0.05 to 1
- wet: int32 [3072, 12288], P('lat', 'lon'), may hold values 0 or 1
- kernel: float32 [384, 384, 768], P('lat', None, 'lon'), may hold values from -0.125 to 0.125
Outputs:
- height_out: float32 [3072, 12288], P('lat', 'lon')
- flux_lon_out: float32 [3072, 12288], P('lat', 'lon')
- flux_lat_out: float32 [3072, 12288], P('lat', 'lon')
- loading_out: float32 [384, 768], P('lat', 'lon')
The draws below stay inside these ranges and needn't reach their ends.
All inputs are finite; a program needn't handle non-finite values. No bound on the sum of `wet` on one device may be relied on, other than what follows from the above.
Results may differ from the reference program's by a relative error of at most 0.00011.
Values sent between devices are 32-bit elements; how exact they have to be, the bound alone decides.
No kernel may reach another device: no remote copies, remote signals or barrier semaphores. Data moves between devices by JAX's collectives and lax.ppermute only.
A program may use at most 128 MiB of HBM per device.

```python
import math
import jax
import jax.numpy as jnp
from jax import lax

STEPS = 2
ROW_RATIO = 8
COL_RATIO = 16
GRID_ROWS = 3072
GRID_COLS = 12288
MASS_ROWS = 384
MASS_COLS = 768


def with_ends(drawn, stream_key, least, largest):
    place = [jax.random.randint(jax.random.fold_in(stream_key, axis), (), 0, length) for axis, length in enumerate(drawn.shape)]
    main_axis = drawn.shape.index(max(drawn.shape))
    next_to = place[:main_axis] + [(place[main_axis] + 1) % drawn.shape[main_axis]] + place[main_axis + 1:]
    return drawn.at[tuple(place)].set(least).at[tuple(next_to)].set(largest)


def shard_levels(own_key, dims, cuts, low, largest):
    factor_of, own = 1.0, jax.random.fold_in(own_key, 6)
    for dim, shards_of in cuts:
        heights = jnp.exp(jax.random.uniform(jax.random.fold_in(own, dim), (shards_of,), jnp.float32, low / len(cuts), largest / len(cuts)))
        factor_of = factor_of * jnp.repeat(heights, dims[dim] // shards_of).reshape([-1 if axis == dim else 1 for axis in range(len(dims))])
    return factor_of


def scatter_about(stream_key, shape, scale, reach, pieces=(), held_as=jnp.bfloat16):
    values = jax.random.normal(stream_key, shape, jnp.float32) * scale
    if len(pieces) > 0:
        values = shard_levels(stream_key, shape, pieces, -0.22, 0.18) * values
    return jnp.clip(values, min=-reach, max=reach).astype(held_as)


def setup_inputs(seed: int = 0) -> dict:
    splits = jax.random.split(jax.random.key(seed), 7)
    return {
        "height": scatter_about(splits[0], (GRID_ROWS, GRID_COLS), 1.0, 6.0, ((0, 16), (1, 32)), jnp.float32),
        "flux_lon": scatter_about(splits[1], (GRID_ROWS, GRID_COLS), 0.3, 4.0, ((0, 16), (1, 32)), jnp.float32),
        "flux_lat": scatter_about(splits[2], (GRID_ROWS, GRID_COLS), 0.3, 4.0, ((0, 16), (1, 32)), jnp.float32),
        "depth": jnp.clip(jnp.exp(math.log(1.0) - 2.9957323 * jax.random.uniform(splits[3], (GRID_ROWS, GRID_COLS), jnp.float32) ** shard_levels(splits[3], (GRID_ROWS, GRID_COLS), ((0, 16), (1, 32)), -0.2, 0.2)), 0.05, 1.0),
        "wet": with_ends((jax.random.randint(splits[4], (GRID_ROWS, GRID_COLS), 0, 8) < 7).astype(jnp.int32), jax.random.fold_in(splits[4], 1), 0, 1),
        "kernel": scatter_about(splits[5], (MASS_ROWS, MASS_ROWS, MASS_COLS), (MASS_ROWS * MASS_COLS // (ROW_RATIO * COL_RATIO)) ** -0.5, 0.125, ((0, 16), (2, 32)), jnp.float32),
    }


angle_step = math.pi / (180.0 * 240.0)
courant_lon = 0.3
courant_lat = 0.3


def coslat(position, total):
    return jnp.cos((position - 0.5 * total) * angle_step)


def convolve(kernel, mass):
    spec_mass = jnp.fft.rfft(mass, axis=1)

    def one_row(kernel_row):
        spec_row = jnp.fft.rfft(kernel_row, axis=1)
        summed = jnp.sum(spec_row * spec_mass, axis=0)
        return jnp.fft.irfft(summed, n=MASS_COLS)

    return lax.map(one_row, kernel).astype(mass.dtype)


def reference(height, flux_lon, flux_lat, depth, wet, kernel):
    wetf = wet.astype(jnp.float32)
    rows = jnp.arange(GRID_ROWS).astype(jnp.float32)
    cos_center = coslat(rows + 0.5, GRID_ROWS)[:, None]
    cos_north = coslat(rows + 1.0, GRID_ROWS)[:, None]
    cos_south = coslat(rows, GRID_ROWS)[:, None]
    zero_row = jnp.zeros((1, GRID_COLS), jnp.float32)
    wet_north = jnp.concatenate([wetf[1:], zero_row], 0)
    depth_north = jnp.concatenate([depth[1:], zero_row], 0)
    wet_east = jnp.roll(wetf, -1, axis=1)
    depth_east = jnp.roll(depth, -1, axis=1)
    loading = jnp.zeros((MASS_ROWS, MASS_COLS), jnp.float32)
    for step_index in range(STEPS):
        weighted = height * wetf * cos_center
        mass = weighted.reshape(MASS_ROWS, ROW_RATIO, MASS_COLS, COL_RATIO).mean(axis=(1, 3))
        loading = convolve(kernel, mass)
        zeta = height + jnp.repeat(jnp.repeat(loading, ROW_RATIO, axis=0), COL_RATIO, axis=1)
        zeta_east = jnp.roll(zeta, -1, axis=1)
        flux_lon = wetf * wet_east * (flux_lon - courant_lon / cos_center * (0.5 * (depth + depth_east)) * (zeta_east - zeta))
        zeta_north = jnp.concatenate([zeta[1:], zero_row], 0)
        flux_lat = wetf * wet_north * (flux_lat - courant_lat * (0.5 * (depth + depth_north)) * (zeta_north - zeta))
        lat_below = jnp.concatenate([zero_row, flux_lat[:-1]], 0)
        lon_west = jnp.roll(flux_lon, 1, axis=1)
        height = wetf * (height - courant_lon / cos_center * (flux_lon - lon_west)
                         - courant_lat / cos_center * (cos_north * flux_lat - cos_south * lat_below))
    return height, flux_lon, flux_lat, loading
```

```python
import math

import jax
import jax.numpy as jnp
import numpy as np
from jax import lax
from jax.experimental import pallas as pl
from jax.experimental.pallas import tpu as pltpu
from jax.sharding import Mesh
from jax.sharding import PartitionSpec as P

ROWS, COLS = 192, 384
EROWS, ECOLS = 200, 512
GRID_ROWS = 3072
NB = 24
HALO_TILES = 17
STEP_ANGLE = math.pi / (180.0 * 240.0)
COURANT = 0.3
F32 = jnp.float32
BF16 = jnp.bfloat16
HIGHEST = lax.Precision.HIGHEST
VM = pl.BlockSpec(memory_space=pltpu.VMEM)


def iota(shape, dim):
    return lax.broadcasted_iota(jnp.int32, shape, dim)


def cos_row(position):
    angle = (position - 0.5 * GRID_ROWS) * STEP_ANGLE
    s = angle * angle
    return 1.0 + s * (-1.0 / 2 + s * (1.0 / 24 + s * (-1.0 / 720 + s * (1.0 / 40320))))


def lat_index():
    return lax.axis_index("zh") * 4 + lax.axis_index("y")


def mass_tile(weighted):
    pick = (iota((COLS, 128), 0) // 16 == iota((COLS, 128), 1)).astype(F32)
    sums = jnp.dot(weighted, pick, precision=HIGHEST, preferred_element_type=F32)
    sums = jnp.sum(sums.reshape(NB, 8, 128), axis=1) * (1.0 / 128.0)
    tile = sums[0:8]
    for q in range(1, 3):
        tile = tile + pltpu.roll(sums[8 * q : 8 * q + 8], 24 * q, 1)
    return tile


def pack_kernel(h_ref, fl_ref, ft_ref, d_ref, wet_ref, mass_ref, east_ref, west_ref, north_ref, south_ref):
    w = wet_ref[...].astype(F32)
    fields = (h_ref[...], fl_ref[...], ft_ref[...], d_ref[...], w)
    row = (lat_index() * ROWS + iota((ROWS, 128), 0)).astype(F32)
    cosc = jnp.concatenate([cos_row(row + 0.5)] * 3, axis=1)
    tile = mass_tile(fields[0] * w * cosc)
    for z in range(16):
        mass_ref[z] = tile
    lane = iota((ROWS, 128), 1)
    east = jnp.zeros((ROWS, 128), F32)
    west = jnp.zeros((ROWS, 128), F32)
    for f, x in enumerate(fields):
        first, last = x[:, :128], x[:, 256:]
        if f:
            first = pltpu.roll(first, 2 * f, 1)
            last = pltpu.roll(last, 128 - 2 * f, 1)
        west = jnp.where((lane >= 2 * f) & (lane < 2 * f + 2), first, west)
        east = jnp.where((lane >= 126 - 2 * f) & (lane < 128 - 2 * f), last, east)
        for t in range(3):
            at = 8 * (3 * f + t)
            north_ref[at : at + 8, :] = x[ROWS - 8 :, 128 * t : 128 * t + 128]
            south_ref[at : at + 8, :] = x[:8, 128 * t : 128 * t + 128]
    east_ref[...] = east
    west_ref[...] = west


def conv_kernel(mt_ref, k_ref, ks_ref, kn_ref, out_ref, m_ref, s_ref):
    core = lax.axis_index("c")
    lane = iota((8, 128), 1)
    m_ref[...] = jnp.zeros_like(m_ref)
    for yl in range(8):
        zh, y = yl // 4, yl % 4
        for q in range(3):
            parts = [None] * 6
            for b in range(32):
                zl, xc = b // 8, b % 8
                src = mt_ref[y * 8 + xc, zh * 4 + zl]
                t, o = divmod(24 * b, 128)
                shift = (24 * b - 24 * q) % 128
                src = pltpu.roll(src, shift, 1) if shift else src
                parts[t] = jnp.where(lane >= o, src, parts[t]) if o else src
                if o + 24 > 128:
                    parts[t + 1] = src
            rows = jnp.concatenate(parts, axis=1)
            m_ref[pl.ds(pl.multiple_of(core * 64 + (yl * 24 + q * 8), 8), 8), :] = rows
    m = m_ref[...]
    mh = m.astype(BF16)
    ml = (m - mh.astype(F32)).astype(BF16)

    def product(wide):
        wh = wide.astype(BF16)
        wl = (wide - wh.astype(F32)).astype(BF16)
        return (
            jnp.dot(wh, mh, preferred_element_type=F32)
            + jnp.dot(wh, ml, preferred_element_type=F32)
            + jnp.dot(wl, mh, preferred_element_type=F32)
        )

    def lagged(first, second):
        total = pltpu.roll(first, 0, 1, stride=1, stride_axis=0) + pltpu.roll(
            second, 24, 1, stride=1, stride_axis=0
        )
        return jnp.sum(total, axis=0, keepdims=True)

    per = 4
    for group in range(NB // per):
        wide = jnp.concatenate(
            [k_ref[s, per * group : per * group + per].reshape(per * NB, 256) for s in range(2)], axis=0
        )
        p = product(wide)
        for i in range(per):
            a = per * group + i
            s_ref[a + 1 : a + 2, :] = lagged(p[NB * i : NB * i + NB], p[NB * (per + i) : NB * (per + i) + NB])
    wide = jnp.concatenate(
        [jnp.concatenate([r[8 * HALO_TILES : 8 * HALO_TILES + 48], r[8 * HALO_TILES + 48 :]], axis=1) for r in (ks_ref, kn_ref)],
        axis=0,
    )
    p = product(wide)
    s_ref[0:1, :] = lagged(p[0:24], p[24:48])
    s_ref[25:26, :] = lagged(p[48:72], p[72:96])
    s_ref[26:32, :] = jnp.zeros((6, 768), F32)
    base = 2 * (lax.axis_index("zl") * 4 + lax.axis_index("x"))
    for k in range(32):
        start = (24 * k - 1) % 768
        t, o = divmod(start, 128)
        message = jnp.zeros((8, 128), F32)
        for q in range(4):
            shift = (26 * q - start) % 128
            piece = pltpu.roll(s_ref[8 * q : 8 * q + 8, 128 * t : 128 * t + 128], shift, 1)
            held = 128 - o
            if held < 26:
                u = (t + 1) % 6
                other = pltpu.roll(s_ref[8 * q : 8 * q + 8, 128 * u : 128 * u + 128], shift, 1)
                piece = jnp.where(lane >= 26 * q + held, other, piece)
            message = piece if q == 0 else jnp.where(lane >= 26 * q, piece, message)
        out_ref[lax.rem(base + k, 32)] = jnp.where(lane < 104, message, 0.0)


def loading_tile(rs_ref):
    parts = [rs_ref[i] for i in range(32)]
    while len(parts) > 1:
        parts = [parts[i] + parts[i + 1] for i in range(0, len(parts), 2)]
    return parts[0]


def spread(tile):
    lane = iota((8, 128), 1)
    sub = iota((8, 128), 0)
    by_q = []
    for q in range(4):
        cols = []
        for t in range(4):
            j = lane + 128 * t
            v = jnp.where(j < 448, jnp.minimum(j // 16, 24) + 1, 0)
            cols.append(jnp.take_along_axis(tile, v + 26 * q, axis=1))
        by_q.append(cols)

    def coarse(a, t):
        q, s = divmod(a, 8)
        return jnp.broadcast_to(by_q[q][t][s : s + 1, :], (8, 128))

    rows = []
    for i in range(25):
        if i < 24:
            rows.append(jnp.concatenate([coarse(i + 1, t) for t in range(4)], axis=1))
        else:
            rows.append(
                jnp.concatenate([jnp.where(sub < 4, coarse(25, t), coarse(0, t)) for t in range(4)], axis=1)
            )
    return jnp.concatenate(rows, axis=0)


def wide4(x):
    return jnp.concatenate([x] * 4, axis=1)


def fine_step(h, fl, ft, d, w, loading):
    r = iota((EROWS, 128), 0)
    row = (lat_index() * ROWS + jnp.where(r < 196, r, r - EROWS)).astype(F32)
    cosc = cos_row(row + 0.5)
    cosn = wide4(cos_row(row + 1.0))
    coss = wide4(cos_row(row))
    ratio = wide4(COURANT / cosc)

    def east(x):
        return pltpu.roll(x, ECOLS - 1, 1)

    def north(x):
        return pltpu.roll(x, EROWS - 1, 0)

    z = h + loading
    fl = w * east(w) * (fl - ratio * (0.5 * (d + east(d))) * (east(z) - z))
    ft = w * north(w) * (ft - COURANT * (0.5 * (d + north(d))) * (north(z) - z))
    h = w * (
        h - ratio * (fl - pltpu.roll(fl, 1, 1)) - ratio * (cosn * ft - coss * pltpu.roll(ft, 1, 0))
    )
    return h, fl, ft, wide4(cosc)


def first_kernel(
    h_ref, fl_ref, ft_ref, d_ref, wet_ref, fe_ref, fw_ref, fs_ref, fn_ref, rs_ref,
    h_out, fl_out, ft_out, d_out, w_out, mass_ref,
):
    lane = iota((ROWS, 128), 1)
    lane8 = iota((8, 128), 1)
    sub8 = iota((8, 128), 0)

    def side(from_east, from_west, f, at):
        e, w = from_east, from_west
        if f:
            e = pltpu.roll(e, 128 - 2 * f, 1)
            w = pltpu.roll(w, 2 * f, 1)
        return jnp.where(at < 2, e, jnp.where(at >= 126, w, 0.0))

    def edge(ref, f):
        tiles = [ref[8 * (3 * f + t) : 8 * (3 * f + t) + 8, :] for t in range(3)]
        return tiles + [side(ref[120:128, :], ref[128:136, :], f, lane8)]

    ext = []
    for f, x in enumerate((h_ref[...], fl_ref[...], ft_ref[...], d_ref[...], wet_ref[...].astype(F32))):
        main = jnp.concatenate([x, side(fe_ref[...], fw_ref[...], f, lane)], axis=1)
        from_south, from_north = edge(fs_ref, f), edge(fn_ref, f)
        tail = jnp.concatenate(
            [jnp.where(sub8 < 4, n, s) for n, s in zip(from_north, from_south)], axis=1
        )
        ext.append(jnp.concatenate([main, tail], axis=0))
    h, fl, ft, d, w = ext
    h, fl, ft, cosc = fine_step(h, fl, ft, d, w, spread(loading_tile(rs_ref)))
    h_out[...] = h
    fl_out[...] = fl
    ft_out[...] = ft
    d_out[...] = d
    w_out[...] = w
    tile = mass_tile((h * w * cosc)[:ROWS, :COLS])
    for z in range(16):
        mass_ref[z] = tile


def last_kernel(h_ref, fl_ref, ft_ref, d_ref, w_ref, rs_ref, h_out, fl_out, ft_out, load_out):
    tile = loading_tile(rs_ref)
    rows = jnp.concatenate([pltpu.roll(tile, 127 - 26 * q, 1) for q in range(4)], axis=0)
    load_out[...] = pltpu.roll(rows, 31, 0)[:NB, :NB]
    h, fl, ft, _ = fine_step(h_ref[...], fl_ref[...], ft_ref[...], d_ref[...], w_ref[...], spread(tile))
    h_out[...] = h[:ROWS, :COLS]
    fl_out[...] = fl[:ROWS, :COLS]
    ft_out[...] = ft[:ROWS, :COLS]


def struct(*shape):
    return jax.ShapeDtypeStruct(shape, F32)


def call(kernel, name, outs, ins, scratch=()):
    return pl.pallas_call(
        kernel,
        name=name,
        out_shape=outs,
        in_specs=[VM] * len(ins),
        out_specs=jax.tree.map(lambda _: VM, outs),
        scratch_shapes=list(scratch),
    )(*ins)


def body(height, flux_lon, flux_lat, depth, wet, kernel):
    LAT, LON = ("zh", "y"), ("zl", "x", "c")
    fields = (height, flux_lon, flux_lat, depth, wet)
    halves = kernel.transpose(0, 2, 1)
    halves = jnp.stack([halves[:, :, :256], halves[:, :, 128:]])
    mass, to_east, to_west, to_north, to_south = call(
        pack_kernel,
        "pack",
        (struct(16, 8, 128), struct(ROWS, 128), struct(ROWS, 128), struct(120, 128), struct(120, 128)),
        fields,
    )
    up = [(i, (i + 1) % 32) for i in range(32)]
    down = [((i + 1) % 32, i) for i in range(32)]
    from_west = lax.ppermute(to_east, LON, up)
    from_east = lax.ppermute(to_west, LON, down)
    k2 = lax.all_to_all(halves, "c", 0, 0, tiled=True)

    def lat_message(rows, at, edge_row):
        k = k2[:, edge_row].reshape(48, 256)
        return jnp.concatenate(
            [rows, from_east[at : at + 8], from_west[at : at + 8], k[:, :128], k[:, 128:]], axis=0
        )

    from_south = lax.ppermute(lat_message(to_north, ROWS - 8, 23), LAT, [(i, i + 1) for i in range(15)])
    from_north = lax.ppermute(lat_message(to_south, 0, 0), LAT, [(i + 1, i) for i in range(15)])

    def loading_parts(mass):
        column = lax.all_to_all(mass, ("zh", "zl"), 0, 0, tiled=True)
        spreadout = jnp.broadcast_to(column.reshape(1, 2, 64, 128), (16, 2, 64, 128)).reshape(32, 64, 128)
        tiles = lax.all_to_all(spreadout, ("y", "x", "c"), 0, 0, tiled=True)
        partial = call(
            conv_kernel,
            "conv",
            struct(32, 8, 128),
            (tiles.reshape(32, 8, 8, 128), k2, from_south, from_north),
            (pltpu.VMEM((256, 768), F32), pltpu.VMEM((32, 768), F32)),
        )
        return lax.all_to_all(partial, LON, 0, 0, tiled=True)

    parts = loading_parts(mass)
    *state, mass = call(
        first_kernel,
        "first",
        (struct(EROWS, ECOLS),) * 5 + (struct(16, 8, 128),),
        fields + (from_east, from_west, from_south, from_north, parts),
    )
    parts = loading_parts(mass)
    return call(
        last_kernel,
        "last",
        (struct(ROWS, COLS),) * 3 + (struct(NB, NB),),
        tuple(state) + (parts,),
    )


def solution(mesh):
    fine = Mesh(np.asarray(mesh.devices).reshape(4, 4, 4, 4, 2), ("zh", "y", "zl", "x", "c"))
    lat, lon = ("zh", "y"), ("zl", "x", "c")
    return jax.shard_map(
        body,
        mesh=fine,
        in_specs=(P(lat, lon),) * 5 + (P(lat, None, lon),),
        out_specs=(P(lat, lon),) * 4,
        check_vma=False,
    )
```

```python
import math

import jax
import jax.numpy as jnp
import numpy as np
from jax import lax
from jax.experimental import pallas as pl
from jax.experimental.pallas import tpu as pltpu
from jax.sharding import Mesh
from jax.sharding import PartitionSpec as P

ROWS, COLS = 192, 384
EROWS, ECOLS = 200, 512
GRID_ROWS = 3072
NB = 24
HALO_TILES = 8
STEP_ANGLE = math.pi / (180.0 * 240.0)
COURANT = 0.3
F32 = jnp.float32
BF16 = jnp.bfloat16
HIGHEST = lax.Precision.HIGHEST
VM = pl.BlockSpec(memory_space=pltpu.VMEM)


def iota(shape, dim):
    return lax.broadcasted_iota(jnp.int32, shape, dim)


def cos_row(position):
    angle = (position - 0.5 * GRID_ROWS) * STEP_ANGLE
    s = angle * angle
    return 1.0 + s * (-1.0 / 2 + s * (1.0 / 24 + s * (-1.0 / 720 + s * (1.0 / 40320))))


def lat_index():
    return lax.axis_index("zh") * 4 + lax.axis_index("y")


def mass_tile(weighted):
    pick = (iota((COLS, 128), 0) // 16 == iota((COLS, 128), 1)).astype(F32)
    sums = jnp.dot(weighted, pick, precision=HIGHEST, preferred_element_type=F32)
    sums = jnp.sum(sums.reshape(NB, 8, 128), axis=1) * (1.0 / 128.0)
    tile = sums[0:8]
    for q in range(1, 3):
        tile = tile + pltpu.roll(sums[8 * q : 8 * q + 8], 24 * q, 1)
    return tile


def mass_kernel(h_ref, wet_ref, mass_ref):
    row = (lat_index() * ROWS + iota((ROWS, 128), 0)).astype(F32)
    cosc = jnp.concatenate([cos_row(row + 0.5)] * 3, axis=1)
    tile = mass_tile(h_ref[...] * wet_ref[...].astype(F32) * cosc)
    for z in range(16):
        mass_ref[z] = tile


def pack_kernel(h_ref, fl_ref, ft_ref, d_ref, wet_ref, east_ref, west_ref, north_ref, south_ref):
    fields = (h_ref[...], fl_ref[...], ft_ref[...], d_ref[...], wet_ref[...].astype(F32))
    lane = iota((ROWS, 128), 1)
    east = jnp.zeros((ROWS, 128), F32)
    west = jnp.zeros((ROWS, 128), F32)
    for f, x in enumerate(fields):
        first, last = x[:, :128], x[:, 256:]
        if f:
            first = pltpu.roll(first, 2 * f, 1)
            last = pltpu.roll(last, 128 - 2 * f, 1)
        west = jnp.where((lane >= 2 * f) & (lane < 2 * f + 2), first, west)
        east = jnp.where((lane >= 126 - 2 * f) & (lane < 128 - 2 * f), last, east)
    east_ref[...] = east
    west_ref[...] = west
    sub = iota((8, 128), 0)
    for t in range(3):
        for out, at, first in ((north_ref, ROWS - 8, 6), (south_ref, 0, 0)):
            group = None
            for f in range(4):
                x = fields[f][at : at + 8, 128 * t : 128 * t + 128]
                shift = (2 * f - first) % 8
                x = pltpu.roll(x, shift, 0) if shift else x
                group = x if f == 0 else jnp.where(sub >= 2 * f, x, group)
            out[8 * t : 8 * t + 8, :] = group
            out[24 + 8 * t : 32 + 8 * t, :] = fields[4][at : at + 8, 128 * t : 128 * t + 128]


def repack_kernel(in_ref, out_ref):
    lane = iota((8, 128), 1)
    for c in range(2):
        parts = [None] * 5
        for n in range(24):
            j, q = divmod(n, 3)
            t, g = divmod(n, 5)
            shift = (24 * g - 24 * q) % 128
            piece = in_ref[8 * c + j]
            piece = pltpu.roll(piece, shift, 1) if shift else piece
            parts[t] = jnp.where(lane >= 24 * g, piece, parts[t]) if g else piece
        for d in range(16):
            for t in range(5):
                out_ref[2 * d + c, :, 128 * t : 128 * t + 128] = parts[t]


def split(x):
    high = x.astype(BF16)
    return high, (x - high.astype(F32)).astype(BF16)


def product(wide, mh, ml):
    wh, wl = split(wide)
    return (
        jnp.dot(wh, mh, preferred_element_type=F32)
        + jnp.dot(wh, ml, preferred_element_type=F32)
        + jnp.dot(wl, mh, preferred_element_type=F32)
    )


def lagged(first, second):
    total = pltpu.roll(first, 0, 1, stride=1, stride_axis=0) + pltpu.roll(
        second, 24, 1, stride=1, stride_axis=0
    )
    return jnp.sum(total, axis=0, keepdims=True)


def conv_rows(mt_ref, k_ref, m_ref, s_ref):
    core = lax.axis_index("c")
    lane = iota((8, 128), 1)
    m_ref[...] = jnp.zeros_like(m_ref)
    for j in range(8):
        zh, y = divmod(j, 4)
        for q in range(3):
            parts = [None] * 6
            for b in range(32):
                zl, xc = divmod(b, 8)
                i, g = divmod(3 * (4 * zh + zl) + q, 5)
                t, o = divmod(24 * b, 128)
                shift = (24 * b - 24 * g) % 128
                src = mt_ref[8 * y + xc, :, 128 * i : 128 * i + 128]
                src = pltpu.roll(src, shift, 1) if shift else src
                parts[t] = jnp.where(lane >= o, src, parts[t]) if o else src
                if o + 24 > 128:
                    parts[t + 1] = src
            at = pl.multiple_of(core * 64 + (24 * j + 8 * q), 8)
            m_ref[pl.ds(at, 8), :] = jnp.concatenate(parts, axis=1)
    mh, ml = split(m_ref[...])
    per = 4
    for group in range(NB // per):
        wide = jnp.concatenate(
            [k_ref[s, per * group : per * group + per].reshape(per * NB, 256) for s in range(2)], axis=0
        )
        p = product(wide, mh, ml)
        for i in range(per):
            a = per * group + i
            s_ref[a + 1 : a + 2, :] = lagged(p[NB * i : NB * i + NB], p[NB * (per + i) : NB * (per + i) + NB])
    return mh, ml


def conv_edges(mh, ml, ks_ref, kn_ref, s_ref, out_ref):
    lane = iota((8, 128), 1)
    wide = jnp.concatenate(
        [jnp.concatenate([r[8 * HALO_TILES : 8 * HALO_TILES + 48], r[8 * HALO_TILES + 48 :]], axis=1) for r in (ks_ref, kn_ref)],
        axis=0,
    )
    p = product(wide, mh, ml)
    s_ref[0:1, :] = lagged(p[0:24], p[24:48])
    s_ref[25:26, :] = lagged(p[48:72], p[72:96])
    s_ref[26:32, :] = jnp.zeros((6, 768), F32)
    base = 2 * (lax.axis_index("zl") * 4 + lax.axis_index("x"))
    for k in range(32):
        start = (24 * k - 1) % 768
        t, o = divmod(start, 128)
        message = jnp.zeros((8, 128), F32)
        for q in range(4):
            shift = (26 * q - start) % 128
            piece = pltpu.roll(s_ref[8 * q : 8 * q + 8, 128 * t : 128 * t + 128], shift, 1)
            held = 128 - o
            if held < 26:
                u = (t + 1) % 6
                other = pltpu.roll(s_ref[8 * q : 8 * q + 8, 128 * u : 128 * u + 128], shift, 1)
                piece = jnp.where(lane >= 26 * q + held, other, piece)
            message = piece if q == 0 else jnp.where(lane >= 26 * q, piece, message)
        out_ref[lax.rem(base + k, 32)] = jnp.where(lane < 104, message, 0.0)


def conv_kernel(mt_ref, k_ref, ks_ref, kn_ref, out_ref, m_ref, s_ref):
    mh, ml = conv_rows(mt_ref, k_ref, m_ref, s_ref)
    conv_edges(mh, ml, ks_ref, kn_ref, s_ref, out_ref)


def own_kernel(mt_ref, k_ref, rows_ref, mh_ref, ml_ref, m_ref, s_ref):
    mh_ref[...], ml_ref[...] = conv_rows(mt_ref, k_ref, m_ref, s_ref)
    rows_ref[...] = s_ref[1:25, :]


def edge_kernel(rows_ref, mh_ref, ml_ref, ks_ref, kn_ref, out_ref, s_ref):
    s_ref[1:25, :] = rows_ref[...]
    conv_edges(mh_ref[...], ml_ref[...], ks_ref, kn_ref, s_ref, out_ref)


def loading_tile(rs_ref):
    parts = [rs_ref[i] for i in range(32)]
    while len(parts) > 1:
        parts = [parts[i] + parts[i + 1] for i in range(0, len(parts), 2)]
    return parts[0]


def spread(tile):
    lane = iota((8, 128), 1)
    sub = iota((8, 128), 0)
    by_q = []
    for q in range(4):
        cols = []
        for t in range(4):
            j = lane + 128 * t
            v = jnp.where(j < 448, jnp.minimum(j // 16, 24) + 1, 0)
            cols.append(jnp.take_along_axis(tile, v + 26 * q, axis=1))
        by_q.append(cols)

    def coarse(a, t):
        q, s = divmod(a, 8)
        return jnp.broadcast_to(by_q[q][t][s : s + 1, :], (8, 128))

    rows = []
    for i in range(25):
        if i < 24:
            rows.append(jnp.concatenate([coarse(i + 1, t) for t in range(4)], axis=1))
        else:
            rows.append(
                jnp.concatenate([jnp.where(sub < 4, coarse(25, t), coarse(0, t)) for t in range(4)], axis=1)
            )
    return jnp.concatenate(rows, axis=0)


def wide4(x):
    return jnp.concatenate([x] * 4, axis=1)


def fine_step(h, fl, ft, d, w, loading):
    r = iota((EROWS, 128), 0)
    row = (lat_index() * ROWS + jnp.where(r < 196, r, r - EROWS)).astype(F32)
    cosc = cos_row(row + 0.5)
    cosn = wide4(cos_row(row + 1.0))
    coss = wide4(cos_row(row))
    ratio = wide4(COURANT / cosc)

    def east(x):
        return pltpu.roll(x, ECOLS - 1, 1)

    def north(x):
        return pltpu.roll(x, EROWS - 1, 0)

    z = h + loading
    fl = w * east(w) * (fl - ratio * (0.5 * (d + east(d))) * (east(z) - z))
    ft = w * north(w) * (ft - COURANT * (0.5 * (d + north(d))) * (north(z) - z))
    h = w * (
        h - ratio * (fl - pltpu.roll(fl, 1, 1)) - ratio * (cosn * ft - coss * pltpu.roll(ft, 1, 0))
    )
    return h, fl, ft, wide4(cosc)


def first_kernel(
    h_ref, fl_ref, ft_ref, d_ref, wet_ref, fe_ref, fw_ref, fs_ref, fn_ref, rs_ref,
    h_out, fl_out, ft_out, d_out, w_out, mass_ref,
):
    lane = iota((ROWS, 128), 1)
    lane8 = iota((8, 128), 1)
    sub8 = iota((8, 128), 0)

    def side(from_east, from_west, f, at):
        e, w = from_east, from_west
        if f:
            e = pltpu.roll(e, 128 - 2 * f, 1)
            w = pltpu.roll(w, 2 * f, 1)
        return jnp.where(at < 2, e, jnp.where(at >= 126, w, 0.0))

    def edge(ref, f, first):
        at = 0 if f < 4 else 24
        tiles = [ref[at + 8 * t : at + 8 * t + 8, :] for t in range(3)]
        shift = (first - 2 * f) % 8 if f < 4 else 0
        tiles = [pltpu.roll(x, shift, 0) for x in tiles] if shift else tiles
        return tiles + [side(ref[48:56, :], ref[56:64, :], f, lane8)]

    ext = []
    for f, x in enumerate((h_ref[...], fl_ref[...], ft_ref[...], d_ref[...], wet_ref[...].astype(F32))):
        main = jnp.concatenate([x, side(fe_ref[...], fw_ref[...], f, lane)], axis=1)
        from_south, from_north = edge(fs_ref, f, 6), edge(fn_ref, f, 0)
        tail = jnp.concatenate(
            [jnp.where(sub8 < 4, n, s) for n, s in zip(from_north, from_south)], axis=1
        )
        ext.append(jnp.concatenate([main, tail], axis=0))
    h, fl, ft, d, w = ext
    h, fl, ft, cosc = fine_step(h, fl, ft, d, w, spread(loading_tile(rs_ref)))
    h_out[...] = h
    fl_out[...] = fl
    ft_out[...] = ft
    d_out[...] = d
    w_out[...] = w
    tile = mass_tile((h * w * cosc)[:ROWS, :COLS])
    for z in range(16):
        mass_ref[z] = tile


def last_kernel(h_ref, fl_ref, ft_ref, d_ref, w_ref, rs_ref, h_out, fl_out, ft_out, load_out):
    tile = loading_tile(rs_ref)
    rows = jnp.concatenate([pltpu.roll(tile, 127 - 26 * q, 1) for q in range(4)], axis=0)
    load_out[...] = pltpu.roll(rows, 31, 0)[:NB, :NB]
    h, fl, ft, _ = fine_step(h_ref[...], fl_ref[...], ft_ref[...], d_ref[...], w_ref[...], spread(tile))
    h_out[...] = h[:ROWS, :COLS]
    fl_out[...] = fl[:ROWS, :COLS]
    ft_out[...] = ft[:ROWS, :COLS]


def struct(*shape):
    return jax.ShapeDtypeStruct(shape, F32)


def call(kernel, name, outs, ins, scratch=()):
    return pl.pallas_call(
        kernel,
        name=name,
        out_shape=outs,
        in_specs=[VM] * len(ins),
        out_specs=jax.tree.map(lambda _: VM, outs),
        scratch_shapes=list(scratch),
    )(*ins)


def body(height, flux_lon, flux_lat, depth, wet, kernel):
    LAT, LON = ("zh", "y"), ("zl", "x", "c")
    fields = (height, flux_lon, flux_lat, depth, wet)
    mass = call(mass_kernel, "mass", struct(16, 8, 128), (height, wet))
    mass, *tied = lax.optimization_barrier((mass, kernel, *fields))
    to_east, to_west, to_north, to_south = call(
        pack_kernel,
        "pack",
        (struct(ROWS, 128), struct(ROWS, 128), struct(48, 128), struct(48, 128)),
        tied[1:],
    )
    from_west = lax.ppermute(to_east, LON, [(i, (i + 1) % 32) for i in range(32)])
    from_east = lax.ppermute(to_west, LON, [((i + 1) % 32, i) for i in range(32)])
    column = lax.all_to_all(mass, ("zh", "zl"), 0, 0, tiled=True)
    turned = tied[0].transpose(0, 2, 1)
    halves = jnp.stack([turned[:, :, :256], turned[:, :, 128:]])
    column, from_west, from_east, halves = lax.optimization_barrier((column, from_west, from_east, halves))
    k2 = lax.all_to_all(halves, "c", 0, 0, tiled=True)

    column = call(repack_kernel, "repack", struct(32, 8, 640), (column,))
    column, k2 = lax.optimization_barrier((column, k2))
    def lat_message(rows, at, edge_row):
        k = k2[:, edge_row].reshape(48, 256)
        return jnp.concatenate(
            [rows, from_east[at : at + 8], from_west[at : at + 8], k[:, :128], k[:, 128:]], axis=0
        )

    from_south = lax.ppermute(lat_message(to_north, ROWS - 8, 23), LAT, [(i, i + 1) for i in range(15)])
    from_north = lax.ppermute(lat_message(to_south, 0, 0), LAT, [(i + 1, i) for i in range(15)])

    tiles = lax.all_to_all(column, ("y", "x", "c"), 0, 0, tiled=True)
    wide, coarse = pltpu.VMEM((256, 768), F32), pltpu.VMEM((32, 768), F32)
    half = jax.ShapeDtypeStruct((256, 768), BF16)
    own = call(own_kernel, "own", (struct(NB, 768), half, half), (tiles, k2), (wide, coarse))
    parts = call(edge_kernel, "edge", struct(32, 8, 128), (*own, from_south, from_north), (coarse,))
    parts = lax.all_to_all(parts, LON, 0, 0, tiled=True)
    *state, mass = call(
        first_kernel,
        "first",
        (struct(EROWS, ECOLS),) * 5 + (struct(16, 8, 128),),
        fields + (from_east, from_west, from_south, from_north, parts),
    )
    column = lax.all_to_all(mass, ("zh", "zl"), 0, 0, tiled=True)
    column = call(repack_kernel, "repack", struct(32, 8, 640), (column,))
    tiles = lax.all_to_all(column, ("y", "x", "c"), 0, 0, tiled=True)
    parts = call(conv_kernel, "conv", struct(32, 8, 128), (tiles, k2, from_south, from_north), (wide, coarse))
    parts = lax.all_to_all(parts, LON, 0, 0, tiled=True)
    return call(
        last_kernel,
        "last",
        (struct(ROWS, COLS),) * 3 + (struct(NB, NB),),
        tuple(state) + (parts,),
    )


def solution(mesh):
    fine = Mesh(np.asarray(mesh.devices).reshape(4, 4, 4, 4, 2), ("zh", "y", "zl", "x", "c"))
    lat, lon = ("zh", "y"), ("zl", "x", "c")
    return jax.shard_map(
        body,
        mesh=fine,
        in_specs=(P(lat, lon),) * 5 + (P(lat, None, lon),),
        out_specs=(P(lat, lon),) * 4,
        check_vma=False,
    )
```

```python
import math

import jax
import jax.numpy as jnp
import numpy as np
from jax import lax
from jax.experimental import pallas as pl
from jax.experimental.pallas import tpu as pltpu
from jax.sharding import Mesh
from jax.sharding import PartitionSpec as P

ROWS, COLS = 192, 384
EROWS, ECOLS = 200, 512
GRID_ROWS = 3072
NB = 24
HALO_TILES = 8
STEP_ANGLE = math.pi / (180.0 * 240.0)
COURANT = 0.3
F32 = jnp.float32
BF16 = jnp.bfloat16
HIGHEST = lax.Precision.HIGHEST
VM = pl.BlockSpec(memory_space=pltpu.VMEM)


def iota(shape, dim):
    return lax.broadcasted_iota(jnp.int32, shape, dim)


def cos_row(position):
    angle = (position - 0.5 * GRID_ROWS) * STEP_ANGLE
    s = angle * angle
    return 1.0 + s * (-1.0 / 2 + s * (1.0 / 24 + s * (-1.0 / 720 + s * (1.0 / 40320))))


def lat_index():
    return lax.axis_index("zh") * 4 + lax.axis_index("y")


def mass_tile(weighted):
    pick = (iota((COLS, 128), 0) // 16 == iota((COLS, 128), 1)).astype(F32)
    sums = jnp.dot(weighted, pick, precision=HIGHEST, preferred_element_type=F32)
    sums = jnp.sum(sums.reshape(NB, 8, 128), axis=1) * (1.0 / 128.0)
    tile = sums[0:8]
    for q in range(1, 3):
        tile = tile + pltpu.roll(sums[8 * q : 8 * q + 8], 24 * q, 1)
    return tile


def mass_kernel(h_ref, wet_ref, mass_ref):
    row = (lat_index() * ROWS + iota((ROWS, 128), 0)).astype(F32)
    cosc = jnp.concatenate([cos_row(row + 0.5)] * 3, axis=1)
    tile = mass_tile(h_ref[...] * wet_ref[...].astype(F32) * cosc)
    for z in range(16):
        mass_ref[z] = tile


def pack_kernel(h_ref, fl_ref, ft_ref, d_ref, wet_ref, east_ref, west_ref, north_ref, south_ref):
    fields = (h_ref[...], fl_ref[...], ft_ref[...], d_ref[...], wet_ref[...].astype(F32))
    lane = iota((ROWS, 128), 1)
    east = jnp.zeros((ROWS, 128), F32)
    west = jnp.zeros((ROWS, 128), F32)
    for f, x in enumerate(fields):
        first, last = x[:, :128], x[:, 256:]
        if f:
            first = pltpu.roll(first, 2 * f, 1)
            last = pltpu.roll(last, 128 - 2 * f, 1)
        west = jnp.where((lane >= 2 * f) & (lane < 2 * f + 2), first, west)
        east = jnp.where((lane >= 126 - 2 * f) & (lane < 128 - 2 * f), last, east)
    east_ref[...] = east
    west_ref[...] = west
    sub = iota((8, 128), 0)
    for t in range(3):
        for out, at, first in ((north_ref, ROWS - 8, 6), (south_ref, 0, 0)):
            group = None
            for f in range(4):
                x = fields[f][at : at + 8, 128 * t : 128 * t + 128]
                shift = (2 * f - first) % 8
                x = pltpu.roll(x, shift, 0) if shift else x
                group = x if f == 0 else jnp.where(sub >= 2 * f, x, group)
            out[8 * t : 8 * t + 8, :] = group
            out[24 + 8 * t : 32 + 8 * t, :] = fields[4][at : at + 8, 128 * t : 128 * t + 128]


def repack_kernel(in_ref, out_ref):
    lane = iota((8, 128), 1)
    for c in range(2):
        parts = [None] * 5
        for n in range(24):
            j, q = divmod(n, 3)
            t, g = divmod(n, 5)
            shift = (24 * g - 24 * q) % 128
            piece = in_ref[8 * c + j]
            piece = pltpu.roll(piece, shift, 1) if shift else piece
            parts[t] = jnp.where(lane >= 24 * g, piece, parts[t]) if g else piece
        for d in range(16):
            for t in range(5):
                out_ref[2 * d + c, :, 128 * t : 128 * t + 128] = parts[t]


def split(x):
    high = x.astype(BF16)
    return high, (x - high.astype(F32)).astype(BF16)


def product(wide, mh, ml):
    wh, wl = split(wide)
    return (
        jnp.dot(wh, mh, preferred_element_type=F32)
        + jnp.dot(wh, ml, preferred_element_type=F32)
        + jnp.dot(wl, mh, preferred_element_type=F32)
    )


def lagged(first, second):
    total = pltpu.roll(first, 0, 1, stride=1, stride_axis=0) + pltpu.roll(
        second, 24, 1, stride=1, stride_axis=0
    )
    return jnp.sum(total, axis=0, keepdims=True)


def by_core(kept, taken):
    front = lax.axis_index("c") == 0
    return jnp.concatenate([jnp.where(front, kept, taken), jnp.where(front, taken, kept)], axis=0)


def conv_rows(mt_ref, kept_ref, taken_ref, m_ref, s_ref):
    core = lax.axis_index("c")
    lane = iota((8, 128), 1)
    m_ref[...] = jnp.zeros_like(m_ref)
    for j in range(8):
        zh, y = divmod(j, 4)
        for q in range(3):
            parts = [None] * 6
            for b in range(32):
                zl, xc = divmod(b, 8)
                i, g = divmod(3 * (4 * zh + zl) + q, 5)
                t, o = divmod(24 * b, 128)
                shift = (24 * b - 24 * g) % 128
                src = mt_ref[8 * y + xc, :, 128 * i : 128 * i + 128]
                src = pltpu.roll(src, shift, 1) if shift else src
                parts[t] = jnp.where(lane >= o, src, parts[t]) if o else src
                if o + 24 > 128:
                    parts[t + 1] = src
            at = pl.multiple_of(core * 64 + (24 * j + 8 * q), 8)
            m_ref[pl.ds(at, 8), :] = jnp.concatenate(parts, axis=1)
    mh, ml = split(m_ref[...])
    per = 4
    for group in range(NB // per):
        wide = by_core(
            *(r[per * group : per * group + per].reshape(per * NB, 256) for r in (kept_ref, taken_ref))
        )
        p = product(wide, mh, ml)
        for i in range(per):
            a = per * group + i
            s_ref[a + 1 : a + 2, :] = lagged(p[NB * i : NB * i + NB], p[NB * (per + i) : NB * (per + i) + NB])
    return mh, ml


def conv_edges(mh, ml, ks_ref, kn_ref, s_ref, out_ref):
    lane = iota((8, 128), 1)
    wide = []
    for ref in (ks_ref, kn_ref):
        at = 8 * HALO_TILES
        rows = jnp.concatenate([ref[at : at + 48, :], ref[at + 48 : at + 96, :]], axis=1)
        wide.append(by_core(rows[:NB], rows[NB:]))
    wide = jnp.concatenate(wide, axis=0)
    p = product(wide, mh, ml)
    s_ref[0:1, :] = lagged(p[0:24], p[24:48])
    s_ref[25:26, :] = lagged(p[48:72], p[72:96])
    s_ref[26:32, :] = jnp.zeros((6, 768), F32)
    base = 2 * (lax.axis_index("zl") * 4 + lax.axis_index("x"))
    for k in range(32):
        start = (24 * k - 1) % 768
        t, o = divmod(start, 128)
        message = jnp.zeros((8, 128), F32)
        for q in range(4):
            shift = (26 * q - start) % 128
            piece = pltpu.roll(s_ref[8 * q : 8 * q + 8, 128 * t : 128 * t + 128], shift, 1)
            held = 128 - o
            if held < 26:
                u = (t + 1) % 6
                other = pltpu.roll(s_ref[8 * q : 8 * q + 8, 128 * u : 128 * u + 128], shift, 1)
                piece = jnp.where(lane >= 26 * q + held, other, piece)
            message = piece if q == 0 else jnp.where(lane >= 26 * q, piece, message)
        out_ref[lax.rem(base + k, 32)] = jnp.where(lane < 104, message, 0.0)


def conv_kernel(mt_ref, kept_ref, taken_ref, ks_ref, kn_ref, out_ref, m_ref, s_ref):
    mh, ml = conv_rows(mt_ref, kept_ref, taken_ref, m_ref, s_ref)
    conv_edges(mh, ml, ks_ref, kn_ref, s_ref, out_ref)


def own_kernel(mt_ref, kept_ref, taken_ref, rows_ref, mh_ref, ml_ref, m_ref, s_ref):
    mh_ref[...], ml_ref[...] = conv_rows(mt_ref, kept_ref, taken_ref, m_ref, s_ref)
    rows_ref[...] = s_ref[1:25, :]


def edge_kernel(rows_ref, mh_ref, ml_ref, ks_ref, kn_ref, out_ref, s_ref):
    s_ref[1:25, :] = rows_ref[...]
    conv_edges(mh_ref[...], ml_ref[...], ks_ref, kn_ref, s_ref, out_ref)


def loading_tile(rs_ref):
    parts = [rs_ref[i] for i in range(32)]
    while len(parts) > 1:
        parts = [parts[i] + parts[i + 1] for i in range(0, len(parts), 2)]
    return parts[0]


def spread(tile):
    lane = iota((8, 128), 1)
    sub = iota((8, 128), 0)
    by_q = []
    for q in range(4):
        cols = []
        for t in range(4):
            j = lane + 128 * t
            v = jnp.where(j < 448, jnp.minimum(j // 16, 24) + 1, 0)
            cols.append(jnp.take_along_axis(tile, v + 26 * q, axis=1))
        by_q.append(cols)

    def coarse(a, t):
        q, s = divmod(a, 8)
        return jnp.broadcast_to(by_q[q][t][s : s + 1, :], (8, 128))

    rows = []
    for i in range(25):
        if i < 24:
            rows.append(jnp.concatenate([coarse(i + 1, t) for t in range(4)], axis=1))
        else:
            rows.append(
                jnp.concatenate([jnp.where(sub < 4, coarse(25, t), coarse(0, t)) for t in range(4)], axis=1)
            )
    return jnp.concatenate(rows, axis=0)


def wide4(x):
    return jnp.concatenate([x] * 4, axis=1)


def fine_step(h, fl, ft, d, w, loading):
    r = iota((EROWS, 128), 0)
    row = (lat_index() * ROWS + jnp.where(r < 196, r, r - EROWS)).astype(F32)
    cosc = cos_row(row + 0.5)
    cosn = wide4(cos_row(row + 1.0))
    coss = wide4(cos_row(row))
    ratio = wide4(COURANT / cosc)

    def east(x):
        return pltpu.roll(x, ECOLS - 1, 1)

    def north(x):
        return pltpu.roll(x, EROWS - 1, 0)

    z = h + loading
    fl = w * east(w) * (fl - ratio * (0.5 * (d + east(d))) * (east(z) - z))
    ft = w * north(w) * (ft - COURANT * (0.5 * (d + north(d))) * (north(z) - z))
    h = w * (
        h - ratio * (fl - pltpu.roll(fl, 1, 1)) - ratio * (cosn * ft - coss * pltpu.roll(ft, 1, 0))
    )
    return h, fl, ft, wide4(cosc)


def first_kernel(
    h_ref, fl_ref, ft_ref, d_ref, wet_ref, fe_ref, fw_ref, fs_ref, fn_ref, rs_ref,
    h_out, fl_out, ft_out, d_out, w_out, mass_ref,
):
    lane = iota((ROWS, 128), 1)
    lane8 = iota((8, 128), 1)
    sub8 = iota((8, 128), 0)

    def side(from_east, from_west, f, at):
        e, w = from_east, from_west
        if f:
            e = pltpu.roll(e, 128 - 2 * f, 1)
            w = pltpu.roll(w, 2 * f, 1)
        return jnp.where(at < 2, e, jnp.where(at >= 126, w, 0.0))

    def edge(ref, f, first):
        at = 0 if f < 4 else 24
        tiles = [ref[at + 8 * t : at + 8 * t + 8, :] for t in range(3)]
        shift = (first - 2 * f) % 8 if f < 4 else 0
        tiles = [pltpu.roll(x, shift, 0) for x in tiles] if shift else tiles
        return tiles + [side(ref[48:56, :], ref[56:64, :], f, lane8)]

    ext = []
    for f, x in enumerate((h_ref[...], fl_ref[...], ft_ref[...], d_ref[...], wet_ref[...].astype(F32))):
        main = jnp.concatenate([x, side(fe_ref[...], fw_ref[...], f, lane)], axis=1)
        from_south, from_north = edge(fs_ref, f, 6), edge(fn_ref, f, 0)
        tail = jnp.concatenate(
            [jnp.where(sub8 < 4, n, s) for n, s in zip(from_north, from_south)], axis=1
        )
        ext.append(jnp.concatenate([main, tail], axis=0))
    h, fl, ft, d, w = ext
    h, fl, ft, cosc = fine_step(h, fl, ft, d, w, spread(loading_tile(rs_ref)))
    h_out[...] = h
    fl_out[...] = fl
    ft_out[...] = ft
    d_out[...] = d
    w_out[...] = w
    tile = mass_tile((h * w * cosc)[:ROWS, :COLS])
    for z in range(16):
        mass_ref[z] = tile


def last_kernel(h_ref, fl_ref, ft_ref, d_ref, w_ref, rs_ref, h_out, fl_out, ft_out, load_out):
    tile = loading_tile(rs_ref)
    rows = jnp.concatenate([pltpu.roll(tile, 127 - 26 * q, 1) for q in range(4)], axis=0)
    load_out[...] = pltpu.roll(rows, 31, 0)[:NB, :NB]
    h, fl, ft, _ = fine_step(h_ref[...], fl_ref[...], ft_ref[...], d_ref[...], w_ref[...], spread(tile))
    h_out[...] = h[:ROWS, :COLS]
    fl_out[...] = fl[:ROWS, :COLS]
    ft_out[...] = ft[:ROWS, :COLS]


def struct(*shape):
    return jax.ShapeDtypeStruct(shape, F32)


def call(kernel, name, outs, ins, scratch=()):
    return pl.pallas_call(
        kernel,
        name=name,
        out_shape=outs,
        in_specs=[VM] * len(ins),
        out_specs=jax.tree.map(lambda _: VM, outs),
        scratch_shapes=list(scratch),
    )(*ins)


def body(height, flux_lon, flux_lat, depth, wet, kernel):
    LAT, LON = ("zh", "y"), ("zl", "x", "c")
    fields = (height, flux_lon, flux_lat, depth, wet)
    mass = call(mass_kernel, "mass", struct(16, 8, 128), (height, wet))
    mass, *tied = lax.optimization_barrier((mass, kernel, *fields))
    to_east, to_west, to_north, to_south = call(
        pack_kernel,
        "pack",
        (struct(ROWS, 128), struct(ROWS, 128), struct(48, 128), struct(48, 128)),
        tied[1:],
    )
    from_west = lax.ppermute(to_east, LON, [(i, (i + 1) % 32) for i in range(32)])
    from_east = lax.ppermute(to_west, LON, [((i + 1) % 32, i) for i in range(32)])
    column = lax.all_to_all(mass, ("zh", "zl"), 0, 0, tiled=True)
    turned = tied[0].transpose(0, 2, 1)
    front = lax.axis_index("c") == 0
    kept = jnp.where(front, turned[:, :, :256], turned[:, :, 128:])
    given = jnp.where(front, turned[:, :, 128:], turned[:, :, :256])
    taken = lax.ppermute(given, "c", [(0, 1), (1, 0)])
    column, from_west, from_east, kept, taken = lax.optimization_barrier(
        (column, from_west, from_east, kept, taken)
    )
    column = call(repack_kernel, "repack", struct(32, 8, 640), (column,))
    def lat_message(rows, at, edge_row):
        k = jnp.concatenate([kept[edge_row], taken[edge_row]], axis=0)
        return jnp.concatenate(
            [rows, from_east[at : at + 8], from_west[at : at + 8], k[:, :128], k[:, 128:]], axis=0
        )

    from_south = lax.ppermute(lat_message(to_north, ROWS - 8, 23), LAT, [(i, i + 1) for i in range(15)])
    from_north = lax.ppermute(lat_message(to_south, 0, 0), LAT, [(i + 1, i) for i in range(15)])

    tiles = lax.all_to_all(column, ("y", "x", "c"), 0, 0, tiled=True)
    wide, coarse = pltpu.VMEM((256, 768), F32), pltpu.VMEM((32, 768), F32)
    half = jax.ShapeDtypeStruct((256, 768), BF16)
    own = call(own_kernel, "own", (struct(NB, 768), half, half), (tiles, kept, taken), (wide, coarse))
    parts = call(edge_kernel, "edge", struct(32, 8, 128), (*own, from_south, from_north), (coarse,))
    parts = lax.all_to_all(parts, LON, 0, 0, tiled=True)
    *state, mass = call(
        first_kernel,
        "first",
        (struct(EROWS, ECOLS),) * 5 + (struct(16, 8, 128),),
        fields + (from_east, from_west, from_south, from_north, parts),
    )
    column = lax.all_to_all(mass, ("zh", "zl"), 0, 0, tiled=True)
    column = call(repack_kernel, "repack", struct(32, 8, 640), (column,))
    tiles = lax.all_to_all(column, ("y", "x", "c"), 0, 0, tiled=True)
    parts = call(conv_kernel, "conv", struct(32, 8, 128), (tiles, kept, taken, from_south, from_north), (wide, coarse))
    parts = lax.all_to_all(parts, LON, 0, 0, tiled=True)
    return call(
        last_kernel,
        "last",
        (struct(ROWS, COLS),) * 3 + (struct(NB, NB),),
        tuple(state) + (parts,),
    )


def solution(mesh):
    fine = Mesh(np.asarray(mesh.devices).reshape(4, 4, 4, 4, 2), ("zh", "y", "zl", "x", "c"))
    lat, lon = ("zh", "y"), ("zl", "x", "c")
    return jax.shard_map(
        body,
        mesh=fine,
        in_specs=(P(lat, lon),) * 5 + (P(lat, None, lon),),
        out_specs=(P(lat, lon),) * 4,
        check_vma=False,
    )
```

```python
import math

import jax
import jax.numpy as jnp
import numpy as np
from jax import lax
from jax.experimental import pallas as pl
from jax.experimental.pallas import tpu as pltpu
from jax.sharding import Mesh
from jax.sharding import PartitionSpec as P

ROWS, COLS = 192, 384
EROWS, ECOLS = 200, 512
GRID_ROWS = 3072
NB = 24
HALO_TILES = 8
STEP_ANGLE = math.pi / (180.0 * 240.0)
COURANT = 0.3
F32 = jnp.float32
BF16 = jnp.bfloat16
HIGHEST = lax.Precision.HIGHEST
VM = pl.BlockSpec(memory_space=pltpu.VMEM)


def iota(shape, dim):
    return lax.broadcasted_iota(jnp.int32, shape, dim)


def cos_row(position):
    angle = (position - 0.5 * GRID_ROWS) * STEP_ANGLE
    s = angle * angle
    return 1.0 + s * (-1.0 / 2 + s * (1.0 / 24 + s * (-1.0 / 720 + s * (1.0 / 40320))))


def lat_index():
    return lax.axis_index("zh") * 4 + lax.axis_index("y")


def mass_tile(weighted):
    pick = (iota((COLS, 128), 0) // 16 == iota((COLS, 128), 1)).astype(F32)
    sums = jnp.dot(weighted, pick, precision=HIGHEST, preferred_element_type=F32)
    sums = jnp.sum(sums.reshape(NB, 8, 128), axis=1) * (1.0 / 128.0)
    tile = sums[0:8]
    for q in range(1, 3):
        tile = tile + pltpu.roll(sums[8 * q : 8 * q + 8], 24 * q, 1)
    return tile


def mass_kernel(h_ref, wet_ref, mass_ref):
    row = (lat_index() * ROWS + iota((ROWS, 128), 0)).astype(F32)
    cosc = jnp.concatenate([cos_row(row + 0.5)] * 3, axis=1)
    tile = mass_tile(h_ref[...] * wet_ref[...].astype(F32) * cosc)
    for z in range(16):
        mass_ref[z] = tile


def pack_kernel(h_ref, fl_ref, ft_ref, d_ref, wet_ref, east_ref, west_ref, north_ref, south_ref):
    fields = (h_ref[...], fl_ref[...], ft_ref[...], d_ref[...], wet_ref[...].astype(F32))
    lane = iota((ROWS, 128), 1)
    east = jnp.zeros((ROWS, 128), F32)
    west = jnp.zeros((ROWS, 128), F32)
    for f, x in enumerate(fields):
        first, last = x[:, :128], x[:, 256:]
        if f:
            first = pltpu.roll(first, 2 * f, 1)
            last = pltpu.roll(last, 128 - 2 * f, 1)
        west = jnp.where((lane >= 2 * f) & (lane < 2 * f + 2), first, west)
        east = jnp.where((lane >= 126 - 2 * f) & (lane < 128 - 2 * f), last, east)
    east_ref[...] = east
    west_ref[...] = west
    sub = iota((8, 128), 0)
    for t in range(3):
        for out, at, first in ((north_ref, ROWS - 8, 6), (south_ref, 0, 0)):
            group = None
            for f in range(4):
                x = fields[f][at : at + 8, 128 * t : 128 * t + 128]
                shift = (2 * f - first) % 8
                x = pltpu.roll(x, shift, 0) if shift else x
                group = x if f == 0 else jnp.where(sub >= 2 * f, x, group)
            out[8 * t : 8 * t + 8, :] = group
            out[24 + 8 * t : 32 + 8 * t, :] = fields[4][at : at + 8, 128 * t : 128 * t + 128]


def repack_kernel(in_ref, out_ref):
    lane = iota((8, 128), 1)
    for c in range(2):
        parts = [None] * 5
        for n in range(24):
            j, q = divmod(n, 3)
            t, g = divmod(n, 5)
            shift = (24 * g - 24 * q) % 128
            piece = in_ref[8 * c + j]
            piece = pltpu.roll(piece, shift, 1) if shift else piece
            parts[t] = jnp.where(lane >= 24 * g, piece, parts[t]) if g else piece
        for d in range(16):
            for t in range(5):
                out_ref[2 * d + c, :, 128 * t : 128 * t + 128] = parts[t]


def split(x):
    high = x.astype(BF16)
    return high, (x - high.astype(F32)).astype(BF16)


def product(wide, mh, ml):
    wh, wl = split(wide)
    return (
        jnp.dot(wh, mh, preferred_element_type=F32)
        + jnp.dot(wh, ml, preferred_element_type=F32)
        + jnp.dot(wl, mh, preferred_element_type=F32)
    )


def lagged(first, second):
    total = pltpu.roll(first, 0, 1, stride=1, stride_axis=0) + pltpu.roll(
        second, 24, 1, stride=1, stride_axis=0
    )
    return jnp.sum(total, axis=0, keepdims=True)


def neighbours(outer, inner):
    odd = lax.rem(lax.axis_index("y"), 2) == 1
    return jnp.where(odd, inner, outer), jnp.where(odd, outer, inner)


def by_core(kept, taken):
    front = lax.axis_index("c") == 0
    return jnp.concatenate([jnp.where(front, kept, taken), jnp.where(front, taken, kept)], axis=0)


def conv_rows(mt_ref, kept_ref, taken_ref, m_ref, s_ref):
    core = lax.axis_index("c")
    lane = iota((8, 128), 1)
    m_ref[...] = jnp.zeros_like(m_ref)
    for j in range(8):
        zh, y = divmod(j, 4)
        for q in range(3):
            parts = [None] * 6
            for b in range(32):
                zl, xc = divmod(b, 8)
                i, g = divmod(3 * (4 * zh + zl) + q, 5)
                t, o = divmod(24 * b, 128)
                shift = (24 * b - 24 * g) % 128
                src = mt_ref[8 * y + xc, :, 128 * i : 128 * i + 128]
                src = pltpu.roll(src, shift, 1) if shift else src
                parts[t] = jnp.where(lane >= o, src, parts[t]) if o else src
                if o + 24 > 128:
                    parts[t + 1] = src
            at = pl.multiple_of(core * 64 + (24 * j + 8 * q), 8)
            m_ref[pl.ds(at, 8), :] = jnp.concatenate(parts, axis=1)
    mh, ml = split(m_ref[...])
    per = 4
    for group in range(NB // per):
        wide = by_core(
            *(r[per * group : per * group + per].reshape(per * NB, 256) for r in (kept_ref, taken_ref))
        )
        p = product(wide, mh, ml)
        for i in range(per):
            a = per * group + i
            s_ref[a + 1 : a + 2, :] = lagged(p[NB * i : NB * i + NB], p[NB * (per + i) : NB * (per + i) + NB])
    return mh, ml


def conv_edges(mh, ml, outer_ref, inner_ref, s_ref, out_ref):
    lane = iota((8, 128), 1)
    wide = []
    at = 8 * HALO_TILES
    for ref in neighbours(outer_ref[at : at + 96, :], inner_ref[at : at + 96, :]):
        rows = jnp.concatenate([ref[:48], ref[48:]], axis=1)
        wide.append(by_core(rows[:NB], rows[NB:]))
    wide = jnp.concatenate(wide, axis=0)
    p = product(wide, mh, ml)
    s_ref[0:1, :] = lagged(p[0:24], p[24:48])
    s_ref[25:26, :] = lagged(p[48:72], p[72:96])
    s_ref[26:32, :] = jnp.zeros((6, 768), F32)
    base = 2 * (lax.axis_index("zl") * 4 + lax.axis_index("x"))
    for k in range(32):
        start = (24 * k - 1) % 768
        t, o = divmod(start, 128)
        message = jnp.zeros((8, 128), F32)
        for q in range(4):
            shift = (26 * q - start) % 128
            piece = pltpu.roll(s_ref[8 * q : 8 * q + 8, 128 * t : 128 * t + 128], shift, 1)
            held = 128 - o
            if held < 26:
                u = (t + 1) % 6
                other = pltpu.roll(s_ref[8 * q : 8 * q + 8, 128 * u : 128 * u + 128], shift, 1)
                piece = jnp.where(lane >= 26 * q + held, other, piece)
            message = piece if q == 0 else jnp.where(lane >= 26 * q, piece, message)
        out_ref[lax.rem(base + k, 32)] = jnp.where(lane < 104, message, 0.0)


def conv_kernel(mt_ref, kept_ref, taken_ref, inner_ref, outer_ref, out_ref, m_ref, s_ref):
    mh, ml = conv_rows(mt_ref, kept_ref, taken_ref, m_ref, s_ref)
    conv_edges(mh, ml, outer_ref, inner_ref, s_ref, out_ref)


def own_kernel(mt_ref, kept_ref, taken_ref, rows_ref, mh_ref, ml_ref, m_ref, s_ref):
    mh_ref[...], ml_ref[...] = conv_rows(mt_ref, kept_ref, taken_ref, m_ref, s_ref)
    rows_ref[...] = s_ref[1:25, :]


def edge_kernel(rows_ref, mh_ref, ml_ref, inner_ref, outer_ref, out_ref, s_ref):
    s_ref[1:25, :] = rows_ref[...]
    conv_edges(mh_ref[...], ml_ref[...], outer_ref, inner_ref, s_ref, out_ref)


def loading_tile(rs_ref):
    parts = [rs_ref[i] for i in range(32)]
    while len(parts) > 1:
        parts = [parts[i] + parts[i + 1] for i in range(0, len(parts), 2)]
    return parts[0]


def spread(tile):
    lane = iota((8, 128), 1)
    sub = iota((8, 128), 0)
    by_q = []
    for q in range(4):
        cols = []
        for t in range(4):
            j = lane + 128 * t
            v = jnp.where(j < 448, jnp.minimum(j // 16, 24) + 1, 0)
            cols.append(jnp.take_along_axis(tile, v + 26 * q, axis=1))
        by_q.append(cols)

    def coarse(a, t):
        q, s = divmod(a, 8)
        return jnp.broadcast_to(by_q[q][t][s : s + 1, :], (8, 128))

    rows = []
    for i in range(25):
        if i < 24:
            rows.append(jnp.concatenate([coarse(i + 1, t) for t in range(4)], axis=1))
        else:
            rows.append(
                jnp.concatenate([jnp.where(sub < 4, coarse(25, t), coarse(0, t)) for t in range(4)], axis=1)
            )
    return jnp.concatenate(rows, axis=0)


def wide4(x):
    return jnp.concatenate([x] * 4, axis=1)


def fine_step(h, fl, ft, d, w, loading):
    r = iota((EROWS, 128), 0)
    row = (lat_index() * ROWS + jnp.where(r < 196, r, r - EROWS)).astype(F32)
    cosc = cos_row(row + 0.5)
    cosn = wide4(cos_row(row + 1.0))
    coss = wide4(cos_row(row))
    ratio = wide4(COURANT / cosc)

    def east(x):
        return pltpu.roll(x, ECOLS - 1, 1)

    def north(x):
        return pltpu.roll(x, EROWS - 1, 0)

    z = h + loading
    fl = w * east(w) * (fl - ratio * (0.5 * (d + east(d))) * (east(z) - z))
    ft = w * north(w) * (ft - COURANT * (0.5 * (d + north(d))) * (north(z) - z))
    h = w * (
        h - ratio * (fl - pltpu.roll(fl, 1, 1)) - ratio * (cosn * ft - coss * pltpu.roll(ft, 1, 0))
    )
    return h, fl, ft, wide4(cosc)


def first_kernel(
    h_ref, fl_ref, ft_ref, d_ref, wet_ref, fe_ref, fw_ref, inner_ref, outer_ref, rs_ref,
    h_out, fl_out, ft_out, d_out, w_out, mass_ref,
):
    lane = iota((ROWS, 128), 1)
    lane8 = iota((8, 128), 1)
    sub8 = iota((8, 128), 0)

    def side(from_east, from_west, f, at):
        e, w = from_east, from_west
        if f:
            e = pltpu.roll(e, 128 - 2 * f, 1)
            w = pltpu.roll(w, 2 * f, 1)
        return jnp.where(at < 2, e, jnp.where(at >= 126, w, 0.0))

    south, north = neighbours(outer_ref[:64, :], inner_ref[:64, :])

    def edge(ref, f, first):
        at = 0 if f < 4 else 24
        tiles = [ref[at + 8 * t : at + 8 * t + 8] for t in range(3)]
        shift = (first - 2 * f) % 8 if f < 4 else 0
        tiles = [pltpu.roll(x, shift, 0) for x in tiles] if shift else tiles
        return tiles + [side(ref[48:56], ref[56:64], f, lane8)]

    ext = []
    for f, x in enumerate((h_ref[...], fl_ref[...], ft_ref[...], d_ref[...], wet_ref[...].astype(F32))):
        main = jnp.concatenate([x, side(fe_ref[...], fw_ref[...], f, lane)], axis=1)
        from_south, from_north = edge(south, f, 6), edge(north, f, 0)
        tail = jnp.concatenate(
            [jnp.where(sub8 < 4, n, s) for n, s in zip(from_north, from_south)], axis=1
        )
        ext.append(jnp.concatenate([main, tail], axis=0))
    h, fl, ft, d, w = ext
    h, fl, ft, cosc = fine_step(h, fl, ft, d, w, spread(loading_tile(rs_ref)))
    h_out[...] = h
    fl_out[...] = fl
    ft_out[...] = ft
    d_out[...] = d
    w_out[...] = w
    tile = mass_tile((h * w * cosc)[:ROWS, :COLS])
    for z in range(16):
        mass_ref[z] = tile


def last_kernel(h_ref, fl_ref, ft_ref, d_ref, w_ref, rs_ref, h_out, fl_out, ft_out, load_out):
    tile = loading_tile(rs_ref)
    rows = jnp.concatenate([pltpu.roll(tile, 127 - 26 * q, 1) for q in range(4)], axis=0)
    load_out[...] = pltpu.roll(rows, 31, 0)[:NB, :NB]
    h, fl, ft, _ = fine_step(h_ref[...], fl_ref[...], ft_ref[...], d_ref[...], w_ref[...], spread(tile))
    h_out[...] = h[:ROWS, :COLS]
    fl_out[...] = fl[:ROWS, :COLS]
    ft_out[...] = ft[:ROWS, :COLS]


def struct(*shape):
    return jax.ShapeDtypeStruct(shape, F32)


def call(kernel, name, outs, ins, scratch=()):
    return pl.pallas_call(
        kernel,
        name=name,
        out_shape=outs,
        in_specs=[VM] * len(ins),
        out_specs=jax.tree.map(lambda _: VM, outs),
        scratch_shapes=list(scratch),
    )(*ins)


def body(height, flux_lon, flux_lat, depth, wet, kernel):
    LAT, LON = ("zh", "y"), ("zl", "x", "c")
    fields = (height, flux_lon, flux_lat, depth, wet)
    mass = call(mass_kernel, "mass", struct(16, 8, 128), (height, wet))
    mass, *tied = lax.optimization_barrier((mass, kernel, *fields))
    to_east, to_west, to_north, to_south = call(
        pack_kernel,
        "pack",
        (struct(ROWS, 128), struct(ROWS, 128), struct(48, 128), struct(48, 128)),
        tied[1:],
    )
    from_west = lax.ppermute(to_east, LON, [(i, (i + 1) % 32) for i in range(32)])
    from_east = lax.ppermute(to_west, LON, [((i + 1) % 32, i) for i in range(32)])
    column = lax.all_to_all(mass, ("zh", "zl"), 0, 0, tiled=True)
    turned = tied[0].transpose(0, 2, 1)
    front = lax.axis_index("c") == 0
    kept = jnp.where(front, turned[:, :, :256], turned[:, :, 128:])
    given = jnp.where(front, turned[:, :, 128:], turned[:, :, :256])
    taken = lax.ppermute(given, "c", [(0, 1), (1, 0)])
    column, from_west, from_east, kept, taken = lax.optimization_barrier(
        (column, from_west, from_east, kept, taken)
    )
    column = call(repack_kernel, "repack", struct(32, 8, 640), (column,))
    def lat_message(rows, at, edge_row):
        k = jnp.concatenate([kept[edge_row], taken[edge_row]], axis=0)
        return jnp.concatenate(
            [rows, from_east[at : at + 8], from_west[at : at + 8], k[:, :128], k[:, 128:]], axis=0
        )

    odd = lax.rem(lax.axis_index("y"), 2) == 1
    up, down = lat_message(to_north, ROWS - 8, 23), lat_message(to_south, 0, 0)
    outer = [(i + a, i + 1 - a) for i in range(1, 15, 2) for a in range(2)]
    inner = [(i + a, i + 1 - a) for i in range(0, 16, 2) for a in range(2)]
    inner = lax.ppermute(jnp.where(odd, down, up), LAT, inner)
    outer = lax.ppermute(jnp.where(odd, up, down), LAT, outer)
    tiles = lax.all_to_all(column, ("y", "x", "c"), 0, 0, tiled=True)
    wide, coarse = pltpu.VMEM((256, 768), F32), pltpu.VMEM((32, 768), F32)
    half = jax.ShapeDtypeStruct((256, 768), BF16)
    own = call(own_kernel, "own", (struct(NB, 768), half, half), (tiles, kept, taken), (wide, coarse))
    parts = call(edge_kernel, "edge", struct(32, 8, 128), (*own, inner, outer), (coarse,))
    parts = lax.all_to_all(parts, LON, 0, 0, tiled=True)
    *state, mass = call(
        first_kernel,
        "first",
        (struct(EROWS, ECOLS),) * 5 + (struct(16, 8, 128),),
        fields + (from_east, from_west, inner, outer, parts),
    )
    column = lax.all_to_all(mass, ("zh", "zl"), 0, 0, tiled=True)
    column = call(repack_kernel, "repack", struct(32, 8, 640), (column,))
    tiles = lax.all_to_all(column, ("y", "x", "c"), 0, 0, tiled=True)
    parts = call(conv_kernel, "conv", struct(32, 8, 128), (tiles, kept, taken, inner, outer), (wide, coarse))
    parts = lax.all_to_all(parts, LON, 0, 0, tiled=True)
    return call(
        last_kernel,
        "last",
        (struct(ROWS, COLS),) * 3 + (struct(NB, NB),),
        tuple(state) + (parts,),
    )


def solution(mesh):
    fine = Mesh(np.asarray(mesh.devices).reshape(4, 4, 4, 4, 2), ("zh", "y", "zl", "x", "c"))
    lat, lon = ("zh", "y"), ("zl", "x", "c")
    return jax.shard_map(
        body,
        mesh=fine,
        in_specs=(P(lat, lon),) * 5 + (P(lat, None, lon),),
        out_specs=(P(lat, lon),) * 4,
        check_vma=False,
    )
```
